32 devices in a mesh: grid: 4 (over y, core), tile: 8 (over z, x).
Axes of the slice: x: 2, y: 2, z: 4, core: 2. Of those that a mesh axis runs over, the one named last changes fastest.
Arguments:
- state_field: float32 [4, 128, 4, 4, 4, 4, 128], P('grid', 'tile'), may hold values from -6 to 6
- levels: int32 [4, 6], P('grid'), may hold values from 1 to 4
- sign_bits: int32 [4], P('grid'), may hold values from 0 to 1
Outputs:
- combined_field: float32 [4, 128, 4, 4, 4, 4, 128], P('grid', 'tile')
The draws below stay inside these ranges and needn't reach their ends.
All inputs are finite; a program needn't handle non-finite values.
Results may differ from the reference program's by a relative error of at most 0.0003.
Values sent between devices are 32-bit elements; how exact they have to be, the bound alone decides.
A program may use at most 64 MiB of HBM per device.

```python
import jax
import jax.numpy as jnp
import numpy as np
from jax import lax

Q = 4
L = 128
STEPS = 4
GRIDS = 4
NX = 128


def set_ends(values, key, low, top_value):
    longest = values.shape.index(max(values.shape))
    spots = []
    for shift in (0, 1):
        where = [jax.random.randint(jax.random.fold_in(key, axis), (), 0, length) for axis, length in enumerate(values.shape)]
        where[longest] = (where[longest] + shift) % values.shape[longest]
        spots.append(tuple(where))
    return values.at[spots[0]].set(low).at[spots[1]].set(top_value)


def block_levels(key, extent, split, low, largest):
    def one(axis_at, parts):
        heights = jax.random.uniform(jax.random.fold_in(jax.random.fold_in(key, 6), axis_at), (parts,), jnp.float32, low / len(split), largest / len(split))
        return jnp.repeat(jnp.exp(heights), extent[axis_at] // parts).reshape((-1,) + (1,) * (len(extent) - axis_at - 1))

    loudness = one(*split[0])
    for cut in split[1:]:
        loudness = loudness * one(*cut)
    return loudness


def bell_draw(own_key, shape, deviation, limit, split=(), dtype=jnp.bfloat16):
    values = deviation * jax.random.normal(own_key, shape, jnp.float32)
    if split:
        values = values * block_levels(own_key, shape, split, -0.22, 0.18)
    return jnp.clip(values, -limit, limit).astype(dtype)


def setup_inputs(seed: int = 0) -> dict:
    splits = jax.random.split(jax.random.key(seed), 4)
    state_field = bell_draw(splits[0], (GRIDS, NX, Q, Q, Q, Q, L), 1.0, 6.0, ((0, 4), (1, 8)), jnp.float32)
    levels = set_ends(jax.random.randint(splits[1], (GRIDS, 6), 1, 5), jax.random.fold_in(splits[1], 1), 1, 4).astype(jnp.int32)
    sign_bits = set_ends(jax.random.randint(splits[2], (GRIDS,), 0, 2), jax.random.fold_in(splits[2], 1), 0, 1).astype(jnp.int32)
    return {"state_field": state_field, "levels": levels, "sign_bits": sign_bits}


def hierarchize(values):
    points = values.shape[0]
    stride = 1
    while stride < points:
        blocks = values.reshape(points // (2 * stride), 2 * stride, -1)
        anchor = blocks[:, 0]
        right = jnp.roll(anchor, -1, 0)
        blocks = blocks.at[:, stride].add(-0.5 * (anchor + right))
        values = blocks.reshape(points, -1)
        stride = stride * 2
    return values


def dehierarchize(values):
    points = values.shape[0]
    stride = points // 2
    while stride >= 1:
        blocks = values.reshape(points // (2 * stride), 2 * stride, -1)
        anchor = blocks[:, 0]
        right = jnp.roll(anchor, -1, 0)
        blocks = blocks.at[:, stride].add(0.5 * (anchor + right))
        values = blocks.reshape(points, -1)
        stride = stride // 2
    return values


def level_depth(points):
    depth_max = points.bit_length() - 1
    position = np.arange(points)
    depth = np.full(points, depth_max)
    for power in range(1, depth_max + 1):
        depth = np.where(position % (2 ** power) == 0, depth_max - power, depth)
    return depth, depth_max


def advance(padded, diffuse, advect):
    centre = padded[1:-1]
    forward = padded[2:]
    backward = padded[:-2]
    result = centre + diffuse[0] * (forward - 2.0 * centre + backward) - advect[0] * (forward * forward - backward * backward) * 0.25
    for dimension in range(1, 6):
        forward = jnp.roll(centre, -1, dimension)
        backward = jnp.roll(centre, 1, dimension)
        result = result + diffuse[dimension] * (forward - 2.0 * centre + backward) - advect[dimension] * (forward * forward - backward * backward) * 0.25
    return result


def reference(state_field, levels, sign_bits):
    points = state_field.shape[1]
    depth_np, depth_max = level_depth(points)
    depth = jnp.asarray(depth_np, jnp.int32)

    def evolve_grid(item):
        values, level_row, sign_bit = item
        rates = jnp.exp2(level_row.astype(jnp.float32) - 4.0)
        diffuse = 0.08 * rates
        advect = 0.05 * rates
        for timestep in range(STEPS):
            padded = jnp.concatenate([values[-1:], values, values[:1]], 0)
            values = advance(padded, diffuse, advect)
        surplus = hierarchize(values.reshape(points, -1))
        sign_value = (2 * sign_bit - 1).astype(jnp.float32)
        return sign_value * surplus

    weighted = lax.map(evolve_grid, (state_field, levels, sign_bits))
    combined = jnp.sum(weighted, 0)

    def rebuild_grid(level_first):
        keep_mask = jnp.where(depth <= depth_max - 4 + level_first, 1.0, 0.0).astype(jnp.float32)
        rebuilt = dehierarchize(keep_mask[:, None] * combined)
        return rebuilt.reshape(state_field.shape[1:])

    return lax.map(rebuild_grid, levels[:, 0])
```

```python
import functools

import jax
import jax.numpy as jnp
from jax import lax
from jax.experimental import pallas as pl
from jax.experimental.pallas import tpu as pltpu
from jax.sharding import PartitionSpec as P

STEPS = 4
ALPHA = 0.08
BETA = 0.0125


def rate_of(level):
    return jnp.where(
        level >= 4, 1.0, jnp.where(level == 3, 0.5, jnp.where(level == 2, 0.25, 0.125))
    ).astype(jnp.float32)


def kernel(
    grids, tiles, X, B,
    levels_ref, sign_ref, x_ref, o_ref,
    u0, halo_l, halo_r, pa, ma, pb, mb, val, from_pair, part, from_far, comb, out,
    load_sem, halo_send, halo_recv, pair_send, pair_recv, far_send, far_recv,
    back_send, back_recv, next_send, next_recv, store_sem,
):
    H = STEPS
    g = lax.axis_index("grid")
    t = lax.axis_index("tile")
    core = g % 2
    pair = g + 1 - 2 * core
    right = (t + 1) % tiles
    left = (t + tiles - 1) % tiles
    far = grids // 2

    def to(grid_at, tile_at):
        return {"grid": grid_at, "tile": tile_at}

    def remote(src, dst, send, recv, where):
        return pltpu.make_async_remote_copy(
            src_ref=src, dst_ref=dst, send_sem=send, recv_sem=recv,
            device_id=where, device_id_type=pl.DeviceIdType.MESH,
        )

    load = pltpu.make_async_copy(x_ref, u0, load_sem)
    load.start()

    barrier = pltpu.get_barrier_semaphore()
    others = [to(g, left), to(g, right), to(pair, t)]
    others += [to((g + 2 * k) % grids, t) for k in range(1, far)]
    for other in others:
        pl.semaphore_signal(barrier, inc=1, device_id=other, device_id_type=pl.DeviceIdType.MESH)
    pl.semaphore_wait(barrier, len(others))

    rightward = remote(x_ref.at[X - H:X], halo_l, halo_send.at[0], halo_recv.at[0], to(g, right))
    rightward.start()
    leftward = remote(x_ref.at[0:H], halo_r, halo_send.at[1], halo_recv.at[1], to(g, left))
    leftward.start()

    rates = [rate_of(levels_ref[0, d]) for d in range(6)]
    total = rates[0] + rates[1] + rates[2] + rates[3] + rates[4] + rates[5]
    centre = 1.0 / (2.0 * ALPHA) - total
    sign = (2 * sign_ref[0] - 1).astype(jnp.float32)

    blocks = 4
    sub = lax.broadcasted_iota(jnp.int32, (B, 8, 128), 1)
    low = sub < 4
    first = sub % 4 == 0
    last = sub % 4 == 3

    def split(u, p_ref, m_ref, layer, rows):
        bent = BETA * u
        p_ref[layer, rows] = u * (ALPHA - bent)
        m_ref[layer, rows] = u * (ALPHA + bent)

    def convert(src, p_ref, m_ref, start, count):
        def body(i, carry):
            layer = i // blocks
            rows = pl.ds(pl.multiple_of((i % blocks) * B, B), B)
            split(src[layer, rows], p_ref, m_ref, layer + start, rows)
            return carry
        lax.fori_loop(0, count * blocks, body, 0)

    def swapped(v):
        pieces = []
        for k in range(0, B, 2):
            pieces += [v[k + 1:k + 2], v[k:k + 1]]
        return jnp.concatenate(pieces, 0)

    def stencil(p_ref, m_ref, layer, block):
        rows = pl.ds(pl.multiple_of(block * B, B), B)
        up = pl.ds(pl.multiple_of(((block + 1) % blocks) * B, B), B)
        down = pl.ds(pl.multiple_of(((block + blocks - 1) % blocks) * B, B), B)
        p = p_ref[layer, rows]
        m = m_ref[layer, rows]
        acc = centre * (p + m)
        acc += rates[0] * (p_ref[layer + 1, rows] + m_ref[layer - 1, rows])
        acc += rates[1] * (p_ref[layer, up] + m_ref[layer, down])
        p2 = jnp.concatenate([p[2:], p[:2]], 0)
        m2 = jnp.concatenate([m[B - 2:], m[:B - 2]], 0)
        acc += rates[2] * (p2 + m2)
        ph = pltpu.roll(p, 4, 1)
        mh = pltpu.roll(m, 4, 1)
        acc += rates[3] * (jnp.where(low, ph, swapped(ph)) + jnp.where(low, swapped(mh), mh))
        p4 = pltpu.roll(jnp.where(first, ph, p), 7, 1)
        m4 = pltpu.roll(jnp.where(last, mh, m), 1, 1)
        acc += rates[4] * (p4 + m4)
        acc += rates[5] * (pltpu.roll(p, 127, 2) + pltpu.roll(m, 1, 2))
        return acc, rows

    state = [(pa, ma), (pb, mb)]

    def step(at, lo, hi):
        src, dst = state[at % 2], state[(at + 1) % 2]

        def body(i, carry):
            layer = i // blocks + (lo + H)
            acc, rows = stencil(*src, layer, i % blocks)
            if at == STEPS - 1:
                val[layer - H, rows] = sign * acc
            else:
                split(acc, *dst, layer, rows)
            return carry
        lax.fori_loop(0, (hi - lo) * blocks, body, 0)

    bases = list(range(H, X - H, H)) + [0, X - H]
    W = H // 2

    def pair_copy(j):
        return remote(
            val.at[pl.ds(bases[j] + (1 - core) * W, W)], from_pair.at[pl.ds(j * W, W)],
            pair_send.at[j], pair_recv.at[j], to(pair, t),
        )

    def far_copy(j, k):
        return remote(
            part.at[pl.ds(j * W, W)], from_far.at[k - 1, pl.ds(j * W, W)],
            far_send.at[k - 1, j], far_recv.at[k - 1, j], to((g + 2 * k) % grids, t),
        )

    def back_copy(j):
        mine = comb.at[pl.ds(bases[j] + core * W, W)]
        return remote(mine, mine, back_send.at[j], back_recv.at[j], to(pair, t))

    def reduce_pair(j):
        pair_copy(j).wait_recv()

        def body(i, carry):
            w = i // blocks
            rows = pl.ds(pl.multiple_of((i % blocks) * B, B), B)
            part[j * W + w, rows] = (
                val[bases[j] + core * W + w, rows] + from_pair[j * W + w, rows]
            )
            return carry
        lax.fori_loop(0, W * blocks, body, 0)
        for k in range(1, far):
            far_copy(j, k).start()

    def reduce_far(j):
        for k in range(1, far):
            far_copy(j, k).wait_recv()

        def body(i, carry):
            w = i // blocks
            rows = pl.ds(pl.multiple_of((i % blocks) * B, B), B)
            summed = part[j * W + w, rows]
            for k in range(1, far):
                summed += from_far[k - 1, j * W + w, rows]
            comb[bases[j] + core * W + w, rows] = summed
            return carry
        lax.fori_loop(0, W * blocks, body, 0)
        back_copy(j).start()

    inner = len(bases) - 2
    load.wait()
    convert(u0, pa, ma, H, X)
    for at in range(STEPS - 1):
        step(at, at + 1, X - at - 1)
    for j in range(inner):
        step(STEPS - 1, bases[j], bases[j] + H)
        pair_copy(j).start()
    for j in range(inner):
        reduce_pair(j)

    rightward.wait_recv()
    convert(halo_l, pa, ma, 0, H)
    for at in range(STEPS):
        step(at, at + 1 - H, at + 1)
    pair_copy(inner).start()
    reduce_pair(inner)

    leftward.wait_recv()
    convert(halo_r, pa, ma, X + H, H)
    for at in range(STEPS):
        step(at, X - at - 1, X - at - 1 + H)
    pair_copy(inner + 1).start()
    reduce_pair(inner + 1)

    for j in range(inner + 1):
        reduce_far(j)
    back_copy(inner).wait_recv()
    following = remote(comb.at[0], comb.at[X], next_send, next_recv, to(g, left))
    following.start()
    reduce_far(inner + 1)
    for j in range(inner + 2):
        if j != inner:
            back_copy(j).wait_recv()
    following.wait_recv()

    level = levels_ref[0, 0]

    def weighted(i, carry):
        layer = i // blocks
        rows = pl.ds(pl.multiple_of((i % blocks) * B, B), B)
        two, four, eight = layer // 2 * 2, layer // 4 * 4, layer // 8 * 8
        anchor = jnp.where(
            level >= 4, layer, jnp.where(level == 3, two, jnp.where(level == 2, four, eight))
        )
        spacing = jnp.where(level >= 4, 1, jnp.where(level == 3, 2, jnp.where(level == 2, 4, 8)))
        weight = (layer - anchor).astype(jnp.float32) * rates[0]
        out[layer, rows] = (1.0 - weight) * comb[anchor, rows] + weight * comb[anchor + spacing, rows]
        return carry

    stores = []
    for j in range(X // H):
        lax.fori_loop(j * H * blocks, (j + 1) * H * blocks, weighted, 0)
        store = pltpu.make_async_copy(
            out.at[pl.ds(j * H, H)], o_ref.at[pl.ds(j * H, H)], store_sem.at[j]
        )
        store.start()
        stores.append(store)

    rightward.wait_send()
    leftward.wait_send()
    for j in range(inner + 2):
        pair_copy(j).wait_send()
        for k in range(1, far):
            far_copy(j, k).wait_send()
        back_copy(j).wait_send()
    following.wait_send()
    for store in stores:
        store.wait()


def solution(mesh):
    grids, tiles = mesh.shape["grid"], mesh.shape["tile"]

    def on_device(state_field, levels, sign_bits):
        X = state_field.shape[1]
        L = state_field.shape[-1]
        V = state_field.size // (X * 8 * L)
        B = V // state_field.shape[2]
        H = STEPS
        N = X // H
        f32 = jnp.float32
        field = (V, 8, L)
        dma = pltpu.SemaphoreType.DMA
        result = pl.pallas_call(
            functools.partial(kernel, grids, tiles, X, B),
            out_shape=jax.ShapeDtypeStruct((X, *field), f32),
            in_specs=[
                pl.BlockSpec(memory_space=pltpu.SMEM),
                pl.BlockSpec(memory_space=pltpu.SMEM),
                pl.BlockSpec(memory_space=pl.ANY),
            ],
            out_specs=pl.BlockSpec(memory_space=pl.ANY),
            scratch_shapes=[
                pltpu.VMEM((X, *field), f32),
                pltpu.VMEM((H, *field), f32),
                pltpu.VMEM((H, *field), f32),
                pltpu.VMEM((X + 2 * H, *field), f32),
                pltpu.VMEM((X + 2 * H, *field), f32),
                pltpu.VMEM((X + 2 * H, *field), f32),
                pltpu.VMEM((X + 2 * H, *field), f32),
                pltpu.VMEM((X, *field), f32),
                pltpu.VMEM((X // 2, *field), f32),
                pltpu.VMEM((X // 2, *field), f32),
                pltpu.VMEM((grids // 2 - 1, X // 2, *field), f32),
                pltpu.VMEM((X + 1, *field), f32),
                pltpu.VMEM((X, *field), f32),
                dma,
                dma((2,)),
                dma((2,)),
                dma((N,)),
                dma((N,)),
                dma((grids // 2 - 1, N)),
                dma((grids // 2 - 1, N)),
                dma((N,)),
                dma((N,)),
                dma,
                dma,
                dma((N,)),
            ],
            compiler_params=pltpu.CompilerParams(
                collective_id=0, has_side_effects=True, vmem_limit_bytes=48 * 1024 * 1024
            ),
        )(levels, sign_bits, state_field.reshape(X, *field))
        return result.reshape(state_field.shape)

    placed = (P("grid", "tile", None, None, None, None, None), P("grid", None), P("grid"))
    return jax.shard_map(
        on_device,
        mesh=mesh,
        in_specs=placed,
        out_specs=P("grid", "tile", None, None, None, None, None),
        check_vma=False,
    )
```

```python
import functools

import jax
import jax.numpy as jnp
from jax import lax
from jax.experimental import pallas as pl
from jax.experimental.pallas import tpu as pltpu
from jax.sharding import PartitionSpec as P

STEPS = 4
ALPHA = 0.08
BETA = 0.0125


def rate_of(level):
    return jnp.where(
        level >= 4, 1.0, jnp.where(level == 3, 0.5, jnp.where(level == 2, 0.25, 0.125))
    ).astype(jnp.float32)


def kernel(
    grids, tiles, X, B,
    levels_hbm, sign_hbm, x_ref, o_ref,
    levels_ref, sign_ref, u0, halo, pa, ma, pb, mb, val, from_pair, part, from_far, comb, after,
    load_sem, halo_send, halo_recv, pair_send, pair_recv, far_send, far_recv,
    back_send, back_recv, next_send, next_recv,
):
    H = STEPS
    g = lax.axis_index("grid")
    t = lax.axis_index("tile")
    core = g % 2
    pair = g + 1 - 2 * core
    right = (t + 1) % tiles
    left = (t + tiles - 1) % tiles
    far = grids // 2

    def to(grid_at, tile_at):
        return {"grid": grid_at, "tile": tile_at}

    def remote(src, dst, send, recv, where):
        return pltpu.make_async_remote_copy(
            src_ref=src, dst_ref=dst, send_sem=send, recv_sem=recv,
            device_id=where, device_id_type=pl.DeviceIdType.MESH,
        )

    load = pltpu.make_async_copy(x_ref, u0, load_sem.at[0])
    load.start()
    load_levels = pltpu.make_async_copy(levels_hbm, levels_ref, load_sem.at[1])
    load_levels.start()
    load_sign = pltpu.make_async_copy(sign_hbm, sign_ref, load_sem.at[2])
    load_sign.start()

    barrier = pltpu.get_barrier_semaphore()
    others = [to(g, left), to(g, right), to(pair, t)]
    others += [to((g + 2 * k) % grids, t) for k in range(1, far)]
    for other in others:
        pl.semaphore_signal(barrier, inc=1, device_id=other, device_id_type=pl.DeviceIdType.MESH)
    pl.semaphore_wait(barrier, len(others))

    lead = t % 2

    def outward(side, k):
        return remote(
            x_ref.at[k + side * (X - 1 - 2 * k)], halo.at[1 - side, k],
            halo_send.at[side, k], halo_recv.at[1 - side, k],
            to(g, (t + tiles - 1 + 2 * side) % tiles),
        )

    for k in range(H):
        outward(lead, k).start()
    for k in range(H):
        outward(1 - lead, k).start()
    load_levels.wait()
    load_sign.wait()

    rates = [rate_of(levels_ref[0, d]) for d in range(6)]
    total = rates[0] + rates[1] + rates[2] + rates[3] + rates[4] + rates[5]
    centre = 1.0 / (2.0 * ALPHA) - total
    sign = (2 * sign_ref[0] - 1).astype(jnp.float32)

    blocks = 4
    sub = lax.broadcasted_iota(jnp.int32, (B, 8, 128), 1)
    low = sub < 4
    first = sub % 4 == 0
    last = sub % 4 == 3

    def split(u, p_ref, m_ref, layer, rows):
        bent = BETA * u
        p_ref[layer, rows] = u * (ALPHA - bent)
        m_ref[layer, rows] = u * (ALPHA + bent)

    def convert(src, p_ref, m_ref, layer):
        def body(i, carry):
            rows = pl.ds(pl.multiple_of(i * B, B), B)
            split(src[rows], p_ref, m_ref, layer, rows)
            return carry
        lax.fori_loop(0, blocks, body, 0)

    sub = lax.broadcasted_iota(jnp.int32, (2, 8, 128), 1)
    low = sub < 4
    first = sub % 4 == 0
    last = sub % 4 == 3
    fine = blocks * blocks

    def swapped(v):
        return jnp.concatenate([v[1:2], v[0:1]], 0)

    def at_rows(i):
        return pl.ds(i * 2, 2)

    def stencil(p_ref, m_ref, layer, i):
        rows = at_rows(i)
        p = p_ref[layer, rows]
        m = m_ref[layer, rows]
        p5 = pltpu.roll(p, 127, 2)
        m5 = pltpu.roll(m, 1, 2)
        acc = centre * (p + m)
        acc += rates[0] * (p_ref[layer + 1, rows] + m_ref[layer - 1, rows])
        i1, i2 = i // blocks * blocks, i % blocks
        acc += rates[1] * (
            p_ref[layer, at_rows((i + blocks) % fine)]
            + m_ref[layer, at_rows((i + fine - blocks) % fine)]
        )
        acc += rates[2] * (
            p_ref[layer, at_rows(i1 + (i2 + 1) % blocks)]
            + m_ref[layer, at_rows(i1 + (i2 + blocks - 1) % blocks)]
        )
        ph = pltpu.roll(p, 4, 1)
        mh = pltpu.roll(m, 4, 1)
        acc += rates[3] * (jnp.where(low, ph, swapped(ph)) + jnp.where(low, swapped(mh), mh))
        p4 = pltpu.roll(jnp.where(first, ph, p), 7, 1)
        m4 = pltpu.roll(jnp.where(last, mh, m), 1, 1)
        acc += rates[4] * (p4 + m4)
        acc += rates[5] * (p5 + m5)
        return acc, rows

    state = [(pa, ma), (pb, mb)]

    def step(at, lo, count):
        src, dst = state[at % 2], state[(at + 1) % 2]

        def body(i, carry):
            layer = i + (lo + H)
            for n in range(fine):
                acc, rows = stencil(*src, layer, n)
                if at == STEPS - 1:
                    val[layer - H, rows] = sign * acc
                else:
                    split(acc, *dst, layer, rows)
            return carry
        lax.fori_loop(0, count, body, 0)

    chunks = [(at, H) for at in range(H, X - H, H)]
    inner = len(chunks)
    W = H // 2
    for side in (lead, 1 - lead):
        for q in range(2):
            near = H - (q + 1) * W
            chunks.append((near + side * (X - W - 2 * near), W))
    half = B * blocks // 2
    mine = pl.ds(pl.multiple_of(core * half, half), half)
    theirs = pl.ds(pl.multiple_of((1 - core) * half, half), half)

    def layers(j):
        return pl.ds(chunks[j][0], chunks[j][1])

    def pair_copy(j):
        return remote(
            val.at[layers(j), theirs], from_pair.at[layers(j)],
            pair_send.at[j], pair_recv.at[j], to(pair, t),
        )

    def far_copy(j, k):
        return remote(
            part.at[layers(j)], from_far.at[k - 1, layers(j)],
            far_send.at[k - 1, j], far_recv.at[k - 1, j], to((g + 2 * k) % grids, t),
        )

    def back_copy(j):
        own = comb.at[layers(j), mine]
        return remote(own, own, back_send.at[j], back_recv.at[j], to(pair, t))

    def reduce_pair(j):
        pair_copy(j).wait_recv()

        def body(w, carry):
            i = chunks[j][0] + w
            part[i] = val[i, mine] + from_pair[i]
            return carry
        lax.fori_loop(0, chunks[j][1], body, 0)
        for k in range(1, far):
            far_copy(j, k).start()

    def reduce_far(j):
        for k in range(1, far):
            far_copy(j, k).wait_recv()

        def body(w, carry):
            i = chunks[j][0] + w
            summed = part[i]
            for k in range(1, far):
                summed += from_far[k - 1, i]
            comb[i, mine] = summed
            return carry
        lax.fori_loop(0, chunks[j][1], body, 0)
        back_copy(j).start()

    def front(side, lo, hi):
        def mirrored(at):
            return at + side * (X - 1 - 2 * at)

        def wave(k, carry):
            outward(1 - side, k).wait_recv()
            convert(halo.at[side, k], pa, ma, H + mirrored(-1 - k))
            for at in range(STEPS):
                step(at, mirrored(at - k), 1)
            return carry
        lax.fori_loop(lo, hi, wave, 0)

    load.wait()

    def convert_all(i, carry):
        convert(u0.at[i], pa, ma, i + H)
        return carry
    lax.fori_loop(0, X, convert_all, 0)

    for at in range(STEPS):
        step(at, at + 1, 3 * H - 2 - 2 * at)
    pair_copy(0).start()
    for j in range(1, inner):
        for at in range(STEPS):
            step(at, chunks[j][0] + H - 1 - at, H)
            if j == 1 and at == 0:
                reduce_pair(0)
        pair_copy(j).start()
        if j > 1:
            reduce_pair(j - 1)
    front(lead, 0, W)
    pair_copy(inner).start()
    reduce_pair(inner - 1)
    front(lead, W, H)
    pair_copy(inner + 1).start()
    reduce_pair(inner)
    front(1 - lead, 0, W)
    pair_copy(inner + 2).start()
    reduce_pair(inner + 1)
    reduce_far(0)
    front(1 - lead, W, H)
    pair_copy(inner + 3).start()
    reduce_pair(inner + 2)
    for j in range(1, inner):
        reduce_far(j)
    reduce_pair(inner + 3)
    reduce_far(inner)
    reduce_far(inner + 1)
    following = remote(comb.at[0], after, next_send, next_recv, to(g, left))
    back_copy(inner + 1).wait_recv()

    @pl.when(lead == 0)
    def _():
        following.start()

    reduce_far(inner + 2)
    reduce_far(inner + 3)
    back_copy(inner + 3).wait_recv()

    @pl.when(lead == 1)
    def _():
        following.start()

    for j in list(range(inner + 1)) + [inner + 2]:
        back_copy(j).wait_recv()

    level = levels_ref[0, 0]

    def weighted(i, carry):
        layer = i // blocks
        rows = pl.ds(pl.multiple_of((i % blocks) * B, B), B)
        two, four, eight = layer // 2 * 2, layer // 4 * 4, layer // 8 * 8
        anchor = jnp.where(
            level >= 4, layer, jnp.where(level == 3, two, jnp.where(level == 2, four, eight))
        )
        spacing = jnp.where(level >= 4, 1, jnp.where(level == 3, 2, jnp.where(level == 2, 4, 8)))
        weight = (layer - anchor).astype(jnp.float32) * rates[0]
        o_ref[layer, rows] = (1.0 - weight) * comb[anchor, rows] + weight * comb[anchor + spacing, rows]
        return carry

    reach = 8
    lax.fori_loop(0, (X - reach) * blocks, weighted, 0)
    following.wait_recv()
    comb[X] = after[...]
    lax.fori_loop((X - reach) * blocks, X * blocks, weighted, 0)

    for k in range(H):
        outward(0, k).wait_send()
        outward(1, k).wait_send()
    for j in range(inner + 4):
        pair_copy(j).wait_send()
        for k in range(1, far):
            far_copy(j, k).wait_send()
        back_copy(j).wait_send()
    following.wait_send()


def solution(mesh):
    grids, tiles = mesh.shape["grid"], mesh.shape["tile"]

    def on_device(state_field, levels, sign_bits):
        X = state_field.shape[1]
        L = state_field.shape[-1]
        V = state_field.size // (X * 8 * L)
        B = V // state_field.shape[2]
        H = STEPS
        N = X // H + 2
        far = grids // 2 - 1
        f32 = jnp.float32
        field = (V, 8, L)
        halved = (V // 2, 8, L)
        dma = pltpu.SemaphoreType.DMA
        result = pl.pallas_call(
            functools.partial(kernel, grids, tiles, X, B),
            out_shape=jax.ShapeDtypeStruct((X, *field), f32),
            in_specs=[pl.BlockSpec(memory_space=pltpu.HBM)] * 3,
            out_specs=pl.BlockSpec(memory_space=pltpu.VMEM),
            scratch_shapes=[
                pltpu.SMEM(levels.shape, jnp.int32),
                pltpu.SMEM(sign_bits.shape, jnp.int32),
                pltpu.VMEM((X, *field), f32),
                pltpu.VMEM((2, H, *field), f32),
                pltpu.VMEM((X + 2 * H, *field), f32),
                pltpu.VMEM((X + 2 * H, *field), f32),
                pltpu.VMEM((X + 2 * H, *field), f32),
                pltpu.VMEM((X + 2 * H, *field), f32),
                pltpu.VMEM((X, *field), f32),
                pltpu.VMEM((X, *halved), f32),
                pltpu.VMEM((X, *halved), f32),
                pltpu.VMEM((far, X, *halved), f32),
                pltpu.VMEM((X + 1, *field), f32),
                pltpu.VMEM(field, f32),
                dma((3,)),
                dma((2, H)),
                dma((2, H)),
                dma((N,)),
                dma((N,)),
                dma((far, N)),
                dma((far, N)),
                dma((N,)),
                dma((N,)),
                dma,
                dma,
            ],
            compiler_params=pltpu.CompilerParams(
                collective_id=0, has_side_effects=True, vmem_limit_bytes=48 * 1024 * 1024
            ),
        )(levels, sign_bits, state_field.reshape(X, *field))
        return result.reshape(state_field.shape)

    placed = (P("grid", "tile", None, None, None, None, None), P("grid", None), P("grid"))
    return jax.shard_map(
        on_device,
        mesh=mesh,
        in_specs=placed,
        out_specs=P("grid", "tile", None, None, None, None, None),
        check_vma=False,
    )
```

```python
import functools

import jax
import jax.numpy as jnp
from jax import lax
from jax.experimental import pallas as pl
from jax.experimental.pallas import tpu as pltpu
from jax.sharding import PartitionSpec as P

STEPS = 4
ALPHA = 0.08
BETA = 0.0125


def rate_of(level):
    return jnp.where(
        level >= 4, 1.0, jnp.where(level == 3, 0.5, jnp.where(level == 2, 0.25, 0.125))
    ).astype(jnp.float32)


def kernel(
    grids, tiles, X, B,
    levels_hbm, sign_hbm, x_ref, o_ref,
    levels_ref, sign_ref, u0, halo, pa, ma, pb, mb, val, from_pair, part, from_far, comb, after,
    load_sem, halo_send, halo_recv, pair_send, pair_recv, far_send, far_recv,
    back_send, back_recv, next_send, next_recv,
):
    H = STEPS
    g = lax.axis_index("grid")
    t = lax.axis_index("tile")
    core = g % 2
    pair = g + 1 - 2 * core
    right = (t + 1) % tiles
    left = (t + tiles - 1) % tiles
    far = grids // 2

    def to(grid_at, tile_at):
        return {"grid": grid_at, "tile": tile_at}

    def remote(src, dst, send, recv, where):
        return pltpu.make_async_remote_copy(
            src_ref=src, dst_ref=dst, send_sem=send, recv_sem=recv,
            device_id=where, device_id_type=pl.DeviceIdType.MESH,
        )

    load = pltpu.make_async_copy(x_ref, u0, load_sem.at[0])
    load.start()
    load_levels = pltpu.make_async_copy(levels_hbm, levels_ref, load_sem.at[1])
    load_levels.start()
    load_sign = pltpu.make_async_copy(sign_hbm, sign_ref, load_sem.at[2])
    load_sign.start()

    barrier = pltpu.get_barrier_semaphore()
    others = [to(g, left), to(g, right), to(pair, t)]
    others += [to((g + 2 * k) % grids, t) for k in range(1, far)]
    for other in others:
        pl.semaphore_signal(barrier, inc=1, device_id=other, device_id_type=pl.DeviceIdType.MESH)
    pl.semaphore_wait(barrier, len(others))

    lead = t % 2

    def outward(side, k):
        return remote(
            x_ref.at[k + side * (X - 1 - 2 * k)], halo.at[1 - side, k],
            halo_send.at[side, k], halo_recv.at[1 - side, k],
            to(g, (t + tiles - 1 + 2 * side) % tiles),
        )

    for k in range(H):
        outward(lead, k).start()
    for k in range(H):
        outward(1 - lead, k).start()
    load_levels.wait()
    load_sign.wait()

    rates = [rate_of(levels_ref[0, d]) for d in range(6)]
    total = rates[0] + rates[1] + rates[2] + rates[3] + rates[4] + rates[5]
    centre = 1.0 / (2.0 * ALPHA) - total
    sign = (2 * sign_ref[0] - 1).astype(jnp.float32)

    blocks = 4
    sub = lax.broadcasted_iota(jnp.int32, (B, 8, 128), 1)
    low = sub < 4
    first = sub % 4 == 0
    last = sub % 4 == 3

    def split(u, p_ref, m_ref, layer, rows):
        bent = BETA * u
        p_ref[layer, rows] = u * (ALPHA - bent)
        m_ref[layer, rows] = u * (ALPHA + bent)

    def convert(src, p_ref, m_ref, layer):
        def body(i, carry):
            rows = pl.ds(pl.multiple_of(i * B, B), B)
            split(src[rows], p_ref, m_ref, layer, rows)
            return carry
        lax.fori_loop(0, blocks, body, 0)

    sub = lax.broadcasted_iota(jnp.int32, (2, 8, 128), 1)
    low = sub < 4
    first = sub % 4 == 0
    last = sub % 4 == 3
    fine = blocks * blocks

    def swapped(v):
        return jnp.concatenate([v[1:2], v[0:1]], 0)

    def at_rows(i):
        return pl.ds(i * 2, 2)

    def stencil(p_ref, m_ref, layer, i):
        rows = at_rows(i)
        p = p_ref[layer, rows]
        m = m_ref[layer, rows]
        p5 = pltpu.roll(p, 127, 2)
        m5 = pltpu.roll(m, 1, 2)
        acc = centre * (p + m)
        acc += rates[0] * (p_ref[layer + 1, rows] + m_ref[layer - 1, rows])
        i1, i2 = i // blocks * blocks, i % blocks
        acc += rates[1] * (
            p_ref[layer, at_rows((i + blocks) % fine)]
            + m_ref[layer, at_rows((i + fine - blocks) % fine)]
        )
        acc += rates[2] * (
            p_ref[layer, at_rows(i1 + (i2 + 1) % blocks)]
            + m_ref[layer, at_rows(i1 + (i2 + blocks - 1) % blocks)]
        )
        ph = pltpu.roll(p, 4, 1)
        mh = pltpu.roll(m, 4, 1)
        acc += rates[3] * (jnp.where(low, ph, swapped(ph)) + jnp.where(low, swapped(mh), mh))
        p4 = pltpu.roll(jnp.where(first, ph, p), 7, 1)
        m4 = pltpu.roll(jnp.where(last, mh, m), 1, 1)
        acc += rates[4] * (p4 + m4)
        acc += rates[5] * (p5 + m5)
        return acc, rows

    state = [(pa, ma), (pb, mb)]

    def step(at, lo, count):
        src, dst = state[at % 2], state[(at + 1) % 2]

        def body(i, carry):
            layer = i + (lo + H)
            for n in range(fine):
                acc, rows = stencil(*src, layer, n)
                if at == STEPS - 1:
                    val[layer - H, rows] = sign * acc
                else:
                    split(acc, *dst, layer, rows)
            return carry
        lax.fori_loop(0, count, body, 0)

    chunks = [(at, H) for at in range(H, X - H, H)]
    inner = len(chunks)
    W = H // 2
    for side in (lead, 1 - lead):
        for q in range(2):
            near = H - (q + 1) * W
            chunks.append((near + side * (X - W - 2 * near), W))
    half = B * blocks // 2
    mine = pl.ds(pl.multiple_of(core * half, half), half)
    theirs = pl.ds(pl.multiple_of((1 - core) * half, half), half)

    def layers(j):
        return pl.ds(chunks[j][0], chunks[j][1])

    def pair_copy(j):
        return remote(
            val.at[layers(j), theirs], from_pair.at[layers(j)],
            pair_send.at[j], pair_recv.at[j], to(pair, t),
        )

    def far_copy(j, k):
        return remote(
            part.at[layers(j)], from_far.at[k - 1, layers(j)],
            far_send.at[k - 1, j], far_recv.at[k - 1, j], to((g + 2 * k) % grids, t),
        )

    def back_copy(j):
        own = comb.at[layers(j), mine]
        return remote(own, own, back_send.at[j], back_recv.at[j], to(pair, t))

    def reduce_pair(j):
        pair_copy(j).wait_recv()

        def body(w, carry):
            i = chunks[j][0] + w
            part[i] = val[i, mine] + from_pair[i]
            return carry
        lax.fori_loop(0, chunks[j][1], body, 0)
        for k in range(1, far):
            far_copy(j, k).start()

    def reduce_far(j):
        for k in range(1, far):
            far_copy(j, k).wait_recv()

        def body(w, carry):
            i = chunks[j][0] + w
            summed = part[i]
            for k in range(1, far):
                summed += from_far[k - 1, i]
            comb[i, mine] = summed
            return carry
        lax.fori_loop(0, chunks[j][1], body, 0)
        back_copy(j).start()

    def front(side, lo, hi):
        def mirrored(at):
            return at + side * (X - 1 - 2 * at)

        def wave(k, carry):
            outward(1 - side, k).wait_recv()
            convert(halo.at[side, k], pa, ma, H + mirrored(-1 - k))
            for at in range(STEPS):
                step(at, mirrored(at - k), 1)
            return carry
        lax.fori_loop(lo, hi, wave, 0)

    load.wait()

    def convert_all(i, carry):
        convert(u0.at[i], pa, ma, i + H)
        return carry
    lax.fori_loop(0, X, convert_all, 0)

    for at in range(STEPS):
        step(at, at + 1, 3 * H - 2 - 2 * at)
    pair_copy(0).start()
    for j in range(1, inner):
        for at in range(STEPS):
            step(at, chunks[j][0] + H - 1 - at, H)
            if j == 1 and at == 0:
                reduce_pair(0)
        pair_copy(j).start()
        if j > 1:
            reduce_pair(j - 1)
    front(lead, 0, W)
    pair_copy(inner).start()
    reduce_pair(inner - 1)
    front(lead, W, H)
    pair_copy(inner + 1).start()
    reduce_pair(inner)
    front(1 - lead, 0, W)
    pair_copy(inner + 2).start()
    reduce_pair(inner + 1)
    reduce_far(0)
    front(1 - lead, W, H)
    pair_copy(inner + 3).start()
    reduce_pair(inner + 2)
    for j in range(1, inner):
        reduce_far(j)
    reduce_pair(inner + 3)
    reduce_far(inner)
    reduce_far(inner + 1)
    following = remote(comb.at[0], after, next_send, next_recv, to(g, left))
    back_copy(inner + 1).wait_recv()

    @pl.when(lead == 0)
    def _():
        following.start()

    reduce_far(inner + 2)
    reduce_far(inner + 3)
    back_copy(inner + 3).wait_recv()

    @pl.when(lead == 1)
    def _():
        following.start()

    for j in list(range(inner + 1)) + [inner + 2]:
        back_copy(j).wait_recv()

    level = levels_ref[0, 0]

    def weighted(i, carry):
        layer = i // blocks
        rows = pl.ds(pl.multiple_of((i % blocks) * B, B), B)
        two, four, eight = layer // 2 * 2, layer // 4 * 4, layer // 8 * 8
        anchor = jnp.where(
            level >= 4, layer, jnp.where(level == 3, two, jnp.where(level == 2, four, eight))
        )
        spacing = jnp.where(level >= 4, 1, jnp.where(level == 3, 2, jnp.where(level == 2, 4, 8)))
        weight = (layer - anchor).astype(jnp.float32) * rates[0]
        o_ref[layer, rows] = (1.0 - weight) * comb[anchor, rows] + weight * comb[anchor + spacing, rows]
        return carry

    reach = 8
    lax.fori_loop(0, (X - reach) * blocks, weighted, 0, unroll=4)
    following.wait_recv()
    comb[X] = after[...]
    lax.fori_loop((X - reach) * blocks, X * blocks, weighted, 0, unroll=4)

    for k in range(H):
        outward(0, k).wait_send()
        outward(1, k).wait_send()
    for j in range(inner + 4):
        pair_copy(j).wait_send()
        for k in range(1, far):
            far_copy(j, k).wait_send()
        back_copy(j).wait_send()
    following.wait_send()


def solution(mesh):
    grids, tiles = mesh.shape["grid"], mesh.shape["tile"]

    def on_device(state_field, levels, sign_bits):
        X = state_field.shape[1]
        L = state_field.shape[-1]
        V = state_field.size // (X * 8 * L)
        B = V // state_field.shape[2]
        H = STEPS
        N = X // H + 2
        far = grids // 2 - 1
        f32 = jnp.float32
        field = (V, 8, L)
        halved = (V // 2, 8, L)
        dma = pltpu.SemaphoreType.DMA
        result = pl.pallas_call(
            functools.partial(kernel, grids, tiles, X, B),
            out_shape=jax.ShapeDtypeStruct((X, *field), f32),
            in_specs=[pl.BlockSpec(memory_space=pltpu.HBM)] * 3,
            out_specs=pl.BlockSpec(memory_space=pltpu.VMEM),
            scratch_shapes=[
                pltpu.SMEM(levels.shape, jnp.int32),
                pltpu.SMEM(sign_bits.shape, jnp.int32),
                pltpu.VMEM((X, *field), f32),
                pltpu.VMEM((2, H, *field), f32),
                pltpu.VMEM((X + 2 * H, *field), f32),
                pltpu.VMEM((X + 2 * H, *field), f32),
                pltpu.VMEM((X + 2 * H, *field), f32),
                pltpu.VMEM((X + 2 * H, *field), f32),
                pltpu.VMEM((X, *field), f32),
                pltpu.VMEM((X, *halved), f32),
                pltpu.VMEM((X, *halved), f32),
                pltpu.VMEM((far, X, *halved), f32),
                pltpu.VMEM((X + 1, *field), f32),
                pltpu.VMEM(field, f32),
                dma((3,)),
                dma((2, H)),
                dma((2, H)),
                dma((N,)),
                dma((N,)),
                dma((far, N)),
                dma((far, N)),
                dma((N,)),
                dma((N,)),
                dma,
                dma,
            ],
            compiler_params=pltpu.CompilerParams(
                collective_id=0, has_side_effects=True, vmem_limit_bytes=48 * 1024 * 1024
            ),
        )(levels, sign_bits, state_field.reshape(X, *field))
        return result.reshape(state_field.shape)

    placed = (P("grid", "tile", None, None, None, None, None), P("grid", None), P("grid"))
    return jax.shard_map(
        on_device,
        mesh=mesh,
        in_specs=placed,
        out_specs=P("grid", "tile", None, None, None, None, None),
        check_vma=False,
    )
```
